32 devices in a mesh: rows: 16 (over z, y, x), cols: 2 (over core).
Axes of the slice: x: 2, y: 2, z: 4, core: 2. Of those that a mesh axis runs over, the one named last changes fastest.
Arguments:
- grad: float32 [6144, 16384], P('rows', 'cols'), may hold values from -200 to 200
- projection: float32 [512, 6144], P(None, 'rows'), may hold values from -1.5 to 1.5
- moment1: float32 [512, 16384], P('rows', 'cols'), may hold values from -6 to 6
- moment2: float32 [512, 16384], P('rows', 'cols'), may hold values from 0.05 to 3
Outputs:
- update: float32 [6144, 16384], P('rows', 'cols')
- moment1_new: float32 [512, 16384], P('rows', 'cols')
- moment2_new: float32 [512, 16384], P('rows', 'cols')
The draws below stay inside these ranges and needn't reach their ends.
All inputs are finite; a program needn't handle non-finite values.
Results may differ from the reference program's by a relative error of at most 0.00007.
Values sent between devices are 32-bit elements; how exact they have to be, the bound alone decides.
A program may use at most 128 MiB of HBM per device.

```python
import math
import jax
import jax.numpy as jnp
from jax import lax

D = 6144
FF = 16384
RANK = 512
STEP = 100


def draw_grad(key, part):
    key_a, key_b = jax.random.split(jax.random.fold_in(key, 11), 2)
    row_pos = jnp.arange(D, dtype=jnp.float32) / (D - 1)
    row_scale = jnp.exp(jnp.log(3.0) * row_pos)
    col_scale = jnp.exp(jax.random.uniform(key_b, (FF,), jnp.float32, 0.0, jnp.log(10.0)))
    noise = jnp.clip(jax.random.normal(key_a, (D, FF), jnp.float32), -4.0, 4.0)
    return noise * row_scale[:, None] * col_scale[None, :]


def draw_projection(key, part):
    key_a, key_b = jax.random.split(jax.random.fold_in(key, 23), 2)
    row_scale = jnp.exp(jax.random.uniform(key_b, (RANK,), jnp.float32, 0.0, jnp.log(10.0)))
    noise = jnp.clip(jax.random.normal(key_a, (RANK, D), jnp.float32), -4.0, 4.0)
    return noise * row_scale[:, None] / (3.0 * jnp.sqrt(float(D)))


def steps_of(own_key, shape, cuts, smallest, top_value):
    gain = 1.0
    for axis_at, shards_of in cuts:
        draws = jax.random.uniform(jax.random.fold_in(jax.random.fold_in(own_key, 6), axis_at), (shards_of,), jnp.float32, smallest / len(cuts), top_value / len(cuts))
        gain = gain * jnp.repeat(jnp.exp(draws), shape[axis_at] // shards_of).reshape((-1,) + (1,) * (len(shape) - 1 - axis_at))
    return gain


def bell_draw(rng, dims, deviation, most, cuts=(), held_as=jnp.bfloat16):
    values = deviation * jax.random.normal(rng, dims, jnp.float32)
    if cuts:
        values = values * steps_of(rng, dims, cuts, -0.22, 0.18)
    return jnp.clip(values, -most, most).astype(held_as)


def setup_inputs(seed: int = 0) -> dict:
    keys = jax.random.split(jax.random.key(seed), 5)
    return {
        "grad": draw_grad(jax.random.fold_in(keys[4], 71), 0),
        "projection": draw_projection(jax.random.fold_in(keys[4], 71), 0),
        "moment1": bell_draw(keys[2], (RANK, FF), 0.5, 6.0, ((0, 16), (1, 2)), jnp.float32),
        "moment2": jnp.clip(jnp.exp(math.log(3.0) - 4.0943445 * jax.random.uniform(keys[3], (RANK, FF), jnp.float32) ** steps_of(keys[3], (RANK, FF), ((0, 16), (1, 2)), -0.2, 0.2)), 0.05, 3.0),
    }


def reference(grad, projection, moment1, moment2):
    total = jnp.sum(grad * grad)
    clip = jnp.minimum(1.0, 0.5 / jnp.sqrt(total / (D * FF) + 1e-06))
    proj = jnp.dot(projection, grad, precision=lax.Precision.HIGHEST, preferred_element_type=jnp.float32) * clip
    moment1_new = 0.9 * moment1 + 0.1 * proj
    moment2_new = 0.999 * moment2 + 0.001 * proj * proj
    first_fix = 1.0 - 0.9 ** STEP
    second_fix = 1.0 - 0.999 ** STEP
    adapted = moment1_new / first_fix / (jnp.sqrt(moment2_new / second_fix) + 1e-08)
    col_adapted = lax.optimization_barrier(jnp.sum(adapted * adapted, axis=0))
    col_proj = lax.optimization_barrier(jnp.sum(proj * proj, axis=0))
    scale = jnp.sqrt(col_adapted / RANK + 1e-06) / jnp.sqrt(col_proj / RANK + 1e-06)
    update = grad * (clip * scale)[None, :]
    return (update, moment1_new, moment2_new)
```

```python
import functools

import jax
import jax.numpy as jnp
from jax import lax
from jax.experimental import pallas as pl
from jax.experimental.pallas import tpu as pltpu
from jax.sharding import PartitionSpec as P

D = 6144
FF = 16384
RANK = 512
STEP = 100
MESH = pl.DeviceIdType.MESH


def kernel(cfg, grad, projection, m1, m2, m1o, m2o, fac, gbuf, pp, part, sq, sqr, col, colr, *rest):
    rows_bits, cols_bits, steps, width, orders, lags, ahead = cfg
    stages = rows_bits
    recv = rest[:stages]
    gsem, psem, ssem, rsem, qssem, qrsem, cssem, crsem = rest[stages:]
    n = 1 << rows_bits
    own = RANK // n
    me = lax.axis_index("rows")
    my_col = lax.axis_index("cols")

    def bit_of(index, bit):
        return lax.rem(lax.div(index, 1 << bit), 2)

    def partner(index, bit):
        return index + (1 - 2 * bit_of(index, bit)) * (1 << bit)

    row_bits = [bit_of(me, b) for b in range(rows_bits)]
    row_partner = [{"rows": partner(me, b)} for b in range(rows_bits)]
    col_partner = [{"cols": partner(my_col, b)} for b in range(cols_bits)]

    def load_grad(t):
        return pltpu.make_async_copy(
            grad.at[:, pl.ds(pl.multiple_of(t * (2 * width), 128), 2 * width)],
            gbuf.at[t],
            gsem.at[t],
        )

    def load_projection(lane, block):
        place = sum(((block >> b) & 1) << (stages - 1 - k) for k, b in enumerate(orders[lane]))
        return pltpu.make_async_copy(
            projection.at[pl.ds(block * own, own)],
            pp.at[lane, pl.ds(place * own, own)],
            psem.at[lane, block],
        )

    load_grad(0).start()
    for lane in range(2):
        for block in range(n):
            load_projection(lane, block).start()

    @pl.loop(1, steps)
    def _(t):
        load_grad(t).start()

    barrier = pltpu.get_barrier_semaphore()
    for to in row_partner + col_partner:
        pl.semaphore_signal(barrier, inc=1, device_id=to, device_id_type=MESH)
    pl.semaphore_wait(barrier, rows_bits + cols_bits)

    kept, sent = [], []
    for lane in range(2):
        at, keeps, sends = 0, [0], []
        for k, b in enumerate(orders[lane]):
            half = RANK >> (k + 1)
            sends.append(pl.multiple_of(at + (1 - row_bits[b]) * half, own))
            at = pl.multiple_of(at + row_bits[b] * half, own)
            keeps.append(at)
        kept.append(keeps)
        sent.append(sends)

    def exchange(t, lane, k):
        half = RANK >> (k + 1)
        return pltpu.make_async_remote_copy(
            src_ref=part.at[t, lane, pl.ds(sent[lane][k], half)],
            dst_ref=recv[k].at[t, lane],
            send_sem=ssem.at[t, lane, k],
            recv_sem=rsem.at[t, lane, k],
            device_id=row_partner[orders[lane][k]],
            device_id_type=MESH,
        )

    def multiply(t):
        for lane in range(2):
            part[t, lane] = jnp.dot(
                pp[lane],
                gbuf[t, :, lane * width : (lane + 1) * width],
                precision=lax.Precision.HIGHEST,
                preferred_element_type=jnp.float32,
            )
            exchange(t, lane, 0).start()

    for lane in range(2):
        for block in range(n):
            load_projection(lane, block).wait()

    @pl.loop(0, ahead)
    def _(t):
        load_grad(t).wait()
        multiply(t)

    def squares(t, total):
        g = gbuf[t]
        g = g.reshape(g.shape[0] // 8, 8, g.shape[1])
        return total + jnp.sum(g * g, axis=0)

    def squares_late(t, total):
        load_grad(t).wait()
        return squares(t, total)

    total = jnp.zeros((8, 2 * width), jnp.float32)
    total = lax.fori_loop(0, ahead, squares, total)
    total = lax.fori_loop(ahead, steps, squares_late, total)
    sq[0] = jnp.zeros((8, width), jnp.float32) + jnp.sum(total)
    for j, to in enumerate(row_partner + col_partner):
        copy = pltpu.make_async_remote_copy(
            src_ref=sq.at[j],
            dst_ref=sqr.at[j],
            send_sem=qssem.at[j],
            recv_sem=qrsem.at[j],
            device_id=to,
            device_id_type=MESH,
        )
        copy.start()
        copy.wait()
        sq[j + 1] = sq[j] + sqr[j]
    last = rows_bits + cols_bits
    first_fix = 1.0 - 0.9**STEP
    second_fix = 1.0 - 0.999**STEP

    def clip_row():
        return jnp.minimum(1.0, 0.5 / jnp.sqrt(sq[last, 0:1, :] / (D * FF) + 1e-06))

    def finish(t, k):
        for lane in range(2):
            exchange(t, lane, k).wait_recv()
            mine = pl.ds(kept[lane][k + 1], RANK >> (k + 1))
            if k + 1 < stages:
                part[t, lane, mine] = part[t, lane, mine] + recv[k][t, lane]
                exchange(t, lane, k + 1).start()
            else:
                proj = (part[t, lane, mine] + recv[k][t, lane]) * clip_row()
                cols = pl.ds(pl.multiple_of(t * (2 * width) + lane * width, 128), width)
                first = 0.9 * m1[:, cols] + 0.1 * proj
                second = 0.999 * m2[:, cols] + 0.001 * proj * proj
                m1o[:, cols] = first
                m2o[:, cols] = second
                adapted = first / first_fix / (jnp.sqrt(second / second_fix) + 1e-08)
                col[0, 0:1, cols] = jnp.sum(adapted * adapted, axis=0, keepdims=True)
                col[0, 1:2, cols] = jnp.sum(proj * proj, axis=0, keepdims=True)

    @pl.loop(ahead, steps + lags[-1])
    def _(t):
        @pl.when(t < steps)
        def _():
            multiply(t)

        for k in range(stages):

            @pl.when((t >= lags[k]) & (t < steps + lags[k]))
            def _():
                finish(t - lags[k], k)

    for j, to in enumerate(row_partner):
        copy = pltpu.make_async_remote_copy(
            src_ref=col.at[j],
            dst_ref=colr.at[j],
            send_sem=cssem.at[j],
            recv_sem=crsem.at[j],
            device_id=to,
            device_id_type=MESH,
        )
        copy.start()
        copy.wait()
        col[j + 1] = col[j] + colr[j]
    clip = jnp.minimum(1.0, 0.5 / jnp.sqrt(sq[last, 0:1, 0:1] / (D * FF) + 1e-06))
    both = col[stages]
    scale = jnp.sqrt(both[0:1] / RANK + 1e-06) / jnp.sqrt(both[1:2] / RANK + 1e-06)
    fac[...] = clip * scale

    @pl.loop(0, steps)
    def _(t):
        for lane in range(2):
            for k in range(stages):
                exchange(t, lane, k).wait_send()


def shards(rows, cols, grad, projection, moment1, moment2):
    depth, span = grad.shape
    rows_bits, cols_bits = rows.bit_length() - 1, cols.bit_length() - 1
    width = 256 if span % 512 == 0 else 128
    steps = span // (2 * width)
    own = RANK // rows
    natural = tuple(range(rows_bits))
    orders = (natural, natural[1::-1] + natural[2:])
    ahead = min(3, steps)
    lags = tuple((ahead, ahead + 2)[min(k, 1)] + max(k - 1, 0) for k in range(rows_bits))
    cfg = (rows_bits, cols_bits, steps, width, orders, lags, ahead)
    last = rows_bits + cols_bits
    f32 = jnp.float32
    vmem = pl.BlockSpec(memory_space=pltpu.VMEM)
    hbm = pl.BlockSpec(memory_space=pl.ANY)
    dma = pltpu.SemaphoreType.DMA
    moment1_new, moment2_new, factor = pl.pallas_call(
        functools.partial(kernel, cfg),
        out_shape=(
            jax.ShapeDtypeStruct((own, span), f32),
            jax.ShapeDtypeStruct((own, span), f32),
            jax.ShapeDtypeStruct((1, span), f32),
        ),
        in_specs=[hbm, hbm, vmem, vmem],
        out_specs=[vmem, vmem, vmem],
        scratch_shapes=[
            pltpu.VMEM((steps, depth, 2 * width), f32),
            pltpu.VMEM((2, RANK, depth), f32),
            pltpu.VMEM((steps, 2, RANK, width), f32),
            pltpu.VMEM((last + 1, 8, width), f32),
            pltpu.VMEM((last, 8, width), f32),
            pltpu.VMEM((rows_bits + 1, 2, span), f32),
            pltpu.VMEM((rows_bits, 2, span), f32),
        ]
        + [pltpu.VMEM((steps, 2, RANK >> (k + 1), width), f32) for k in range(rows_bits)]
        + [
            dma((steps,)),
            dma((2, rows)),
            dma((steps, 2, rows_bits)),
            dma((steps, 2, rows_bits)),
            dma((last,)),
            dma((last,)),
            dma((rows_bits,)),
            dma((rows_bits,)),
        ],
        compiler_params=pltpu.CompilerParams(
            collective_id=0, has_side_effects=True, vmem_limit_bytes=67000000
        ),
        name="project_reduce",
    )(grad, projection, moment1, moment2)
    return (grad * factor, moment1_new, moment2_new)


def solution(mesh):
    rows, cols = mesh.shape["rows"], mesh.shape["cols"]
    return jax.shard_map(
        functools.partial(shards, rows, cols),
        mesh=mesh,
        in_specs=(P("rows", "cols"), P(None, "rows"), P("rows", "cols"), P("rows", "cols")),
        out_specs=(P("rows", "cols"), P("rows", "cols"), P("rows", "cols")),
        check_vma=False,
    )
```

```python
import functools

import jax
import jax.numpy as jnp
from jax import lax
from jax.experimental import pallas as pl
from jax.experimental.pallas import tpu as pltpu
from jax.sharding import PartitionSpec as P

D = 6144
FF = 16384
RANK = 512
STEP = 100
MESH = pl.DeviceIdType.MESH


def kernel(cfg, grad, projection, m1, m2, m1o, m2o, fac, gbuf, pp, sq, sqr, col, colr, *rest):
    rows_bits, cols_bits, steps, width, orders, plan, lags, ahead = cfg
    stages = rows_bits
    turns = len(plan)
    lanes = [(u, i) for u in range(turns) for i in range(len(plan[u]))]
    bufs = {lane: rest[at * (stages + 1) : (at + 1) * (stages + 1)] for at, lane in enumerate(lanes)}
    number = {lane: at for at, lane in enumerate(lanes)}
    gsem, psem, ssem, rsem, qssem, qrsem, cssem, crsem = rest[len(lanes) * (stages + 1) :]
    n = 1 << rows_bits
    own = RANK // n
    me = lax.axis_index("rows")
    my_col = lax.axis_index("cols")

    def bit_of(index, bit):
        return lax.rem(lax.div(index, 1 << bit), 2)

    def partner(index, bit):
        return index + (1 - 2 * bit_of(index, bit)) * (1 << bit)

    row_bits = [bit_of(me, b) for b in range(rows_bits)]
    row_partner = [{"rows": partner(me, b)} for b in range(rows_bits)]
    col_partner = [{"cols": partner(my_col, b)} for b in range(cols_bits)]

    def load_grad(t):
        return pltpu.make_async_copy(
            grad.at[:, pl.ds(pl.multiple_of(t * width, 128), width)],
            gbuf.at[t],
            gsem.at[t],
        )

    def load_projection(lane, block):
        place = sum(((block >> b) & 1) << (stages - 1 - k) for k, b in enumerate(orders[lane]))
        return pltpu.make_async_copy(
            projection.at[pl.ds(block * own, own)],
            pp.at[lane, pl.ds(place * own, own)],
            psem.at[lane, block],
        )

    load_grad(0).start()
    for lane in range(len(orders)):
        for block in range(n):
            load_projection(lane, block).start()

    @pl.loop(1, steps)
    def _(t):
        load_grad(t).start()

    barrier = pltpu.get_barrier_semaphore()
    for to in row_partner + col_partner:
        pl.semaphore_signal(barrier, inc=1, device_id=to, device_id_type=MESH)
    pl.semaphore_wait(barrier, rows_bits + cols_bits)

    kept, sent = [], []
    for lane in range(len(orders)):
        at, keeps, sends = 0, [0], []
        for k, b in enumerate(orders[lane]):
            half = RANK >> (k + 1)
            sends.append(pl.multiple_of(at + (1 - row_bits[b]) * half, own))
            at = pl.multiple_of(at + row_bits[b] * half, own)
            keeps.append(at)
        kept.append(keeps)
        sent.append(sends)

    def exchange(p, lane, k):
        kind = plan[lane[0]][lane[1]][0]
        half = RANK >> (k + 1)
        return pltpu.make_async_remote_copy(
            src_ref=bufs[lane][0].at[p, pl.ds(sent[kind][k], half)],
            dst_ref=bufs[lane][k + 1].at[p],
            send_sem=ssem.at[number[lane], p, k],
            recv_sem=rsem.at[number[lane], p, k],
            device_id=row_partner[orders[kind][k]],
            device_id_type=MESH,
        )

    def multiply(p, u):
        for i, (kind, at, wide) in enumerate(plan[u]):
            bufs[u, i][0][p] = jnp.dot(
                pp[kind],
                gbuf[p * turns + u, :, at : at + wide],
                precision=lax.Precision.HIGHEST,
                preferred_element_type=jnp.float32,
            )
            exchange(p, (u, i), 0).start()

    for lane in range(len(orders)):
        for block in range(n):
            load_projection(lane, block).wait()

    for t in range(ahead):
        load_grad(t).wait()
        multiply(t // turns, t % turns)

    def squares(t, total):
        g = gbuf[t]
        g = g.reshape(g.shape[0] // 8, 8, g.shape[1])
        return total + jnp.sum(g * g, axis=0)

    def squares_late(t, total):
        load_grad(t).wait()
        return squares(t, total)

    total = jnp.zeros((8, width), jnp.float32)
    total = lax.fori_loop(0, ahead, squares, total)
    total = lax.fori_loop(ahead, steps, squares_late, total)
    sq[0] = jnp.zeros(sq.shape[1:], jnp.float32) + jnp.sum(total)
    for j, to in enumerate(row_partner + col_partner):
        copy = pltpu.make_async_remote_copy(
            src_ref=sq.at[j],
            dst_ref=sqr.at[j],
            send_sem=qssem.at[j],
            recv_sem=qrsem.at[j],
            device_id=to,
            device_id_type=MESH,
        )
        copy.start()
        copy.wait()
        sq[j + 1] = sq[j] + sqr[j]
    last = rows_bits + cols_bits
    first_fix = 1.0 - 0.9**STEP
    second_fix = 1.0 - 0.999**STEP

    def clip_row(wide):
        return jnp.minimum(1.0, 0.5 / jnp.sqrt(sq[last, 0:1, :wide] / (D * FF) + 1e-06))

    def finish(p, u, k):
        for i, (kind, at, wide) in enumerate(plan[u]):
            part, recv = bufs[u, i][0], bufs[u, i][k + 1]
            exchange(p, (u, i), k).wait_recv()
            mine = pl.ds(kept[kind][k + 1], RANK >> (k + 1))
            if k + 1 < stages:
                part[p, mine] = part[p, mine] + recv[p]
                exchange(p, (u, i), k + 1).start()
            else:
                proj = (part[p, mine] + recv[p]) * clip_row(wide)
                cols = pl.ds(pl.multiple_of((p * turns + u) * width + at, 128), wide)
                first = 0.9 * m1[:, cols] + 0.1 * proj
                second = 0.999 * m2[:, cols] + 0.001 * proj * proj
                m1o[:, cols] = first
                m2o[:, cols] = second
                adapted = first / first_fix / (jnp.sqrt(second / second_fix) + 1e-08)
                h = lax.div(p, steps // turns // 2)
                cols = pl.ds(pl.multiple_of((p * turns + u) * width + at - h * col.shape[-1], 128), wide)
                col[0, h, 0:1, cols] = jnp.sum(adapted * adapted, axis=0, keepdims=True)
                col[0, h, 1:2, cols] = jnp.sum(proj * proj, axis=0, keepdims=True)

    @pl.loop(ahead // turns, -(-(steps + lags[-1]) // turns))
    def _(p):
        for u in range(turns):

            @pl.when(p * turns + u < steps)
            def _():
                multiply(p, u)

            for k in range(stages):
                from_u = (u - lags[k]) % turns
                back = p + (u - lags[k] - from_u) // turns

                @pl.when((back >= 0) & (back * turns + from_u < steps))
                def _():
                    finish(back, from_u, k)

    natural = list(range(rows_bits))
    turned = natural[rows_bits // 2 :] + natural[: rows_bits // 2]
    for j in range(rows_bits):
        copies = []
        for h, order in enumerate((natural, turned)):
            copies.append(
                pltpu.make_async_remote_copy(
                    src_ref=col.at[j, h],
                    dst_ref=colr.at[j, h],
                    send_sem=cssem.at[j, h],
                    recv_sem=crsem.at[j, h],
                    device_id=row_partner[order[j]],
                    device_id_type=MESH,
                )
            )
            copies[-1].start()
        for h in range(2):
            copies[h].wait()
            col[j + 1, h] = col[j, h] + colr[j, h]
    clip = jnp.minimum(1.0, 0.5 / jnp.sqrt(sq[last, 0:1, 0:1] / (D * FF) + 1e-06))
    half = col.shape[-1]
    for h in range(2):
        both = col[stages, h]
        scale = jnp.sqrt(both[0:1] / RANK + 1e-06) / jnp.sqrt(both[1:2] / RANK + 1e-06)
        fac[:, h * half : (h + 1) * half] = clip * scale

    @pl.loop(0, steps // turns)
    def _(p):
        for lane in lanes:
            for k in range(stages):
                exchange(p, lane, k).wait_send()


def shards(rows, cols, grad, projection, moment1, moment2):
    depth, span = grad.shape
    rows_bits, cols_bits = rows.bit_length() - 1, cols.bit_length() - 1
    width, turns = 512, 2
    steps = span // width
    own = RANK // rows
    natural = tuple(range(rows_bits))
    orders = (natural, natural[1::-1] + natural[2:], natural[2:] + natural[:2])
    plan = (((0, 0, 128), (1, 128, 128), (2, 256, 256)), ((0, 0, 256), (1, 256, 256)))
    ahead = 2
    lags = tuple(ahead + 2 * k for k in range(rows_bits))
    cfg = (rows_bits, cols_bits, steps, width, orders, plan, lags, ahead)
    pairs = steps // turns
    most = max(wide for turn in plan for _, _, wide in turn)
    last = rows_bits + cols_bits
    f32 = jnp.float32
    vmem = pl.BlockSpec(memory_space=pltpu.VMEM)
    hbm = pl.BlockSpec(memory_space=pl.ANY)
    dma = pltpu.SemaphoreType.DMA
    moment1_new, moment2_new, factor = pl.pallas_call(
        functools.partial(kernel, cfg),
        out_shape=(
            jax.ShapeDtypeStruct((own, span), f32),
            jax.ShapeDtypeStruct((own, span), f32),
            jax.ShapeDtypeStruct((1, span), f32),
        ),
        in_specs=[hbm, hbm, vmem, vmem],
        out_specs=[vmem, vmem, vmem],
        scratch_shapes=[
            pltpu.VMEM((steps, depth, width), f32),
            pltpu.VMEM((len(orders), RANK, depth), f32),
            pltpu.VMEM((last + 1, 8, most), f32),
            pltpu.VMEM((last, 8, most), f32),
            pltpu.VMEM((rows_bits + 1, 2, 2, span // 2), f32),
            pltpu.VMEM((rows_bits, 2, 2, span // 2), f32),
        ]
        + [
            pltpu.VMEM((pairs, RANK >> k, wide), f32)
            for turn in plan
            for _, _, wide in turn
            for k in range(rows_bits + 1)
        ]
        + [
            dma((steps,)),
            dma((len(orders), rows)),
            dma((sum(map(len, plan)), pairs, rows_bits)),
            dma((sum(map(len, plan)), pairs, rows_bits)),
            dma((last,)),
            dma((last,)),
            dma((rows_bits, 2)),
            dma((rows_bits, 2)),
        ],
        compiler_params=pltpu.CompilerParams(
            collective_id=0, has_side_effects=True, vmem_limit_bytes=67000000
        ),
        name="project_reduce",
    )(grad, projection, moment1, moment2)
    return (grad * factor, moment1_new, moment2_new)


def solution(mesh):
    rows, cols = mesh.shape["rows"], mesh.shape["cols"]
    return jax.shard_map(
        functools.partial(shards, rows, cols),
        mesh=mesh,
        in_specs=(P("rows", "cols"), P(None, "rows"), P("rows", "cols"), P("rows", "cols")),
        out_specs=(P("rows", "cols"), P("rows", "cols"), P("rows", "cols")),
        check_vma=False,
    )
```
